32 devices in a mesh: grp: 2 (over x), chan: 16 (over z, y, core).
Axes of the slice: x: 2, y: 2, z: 4, core: 2. Of those that a mesh axis runs over, the one named last changes fastest.
Arguments:
- voltages: bfloat16 [8, 16384, 2048], P('grp', 'chan'), parts along dimension 0, may hold values from -6 to 6
- delay_step: int32 [16384], replicated, may hold values from 0 to 1048575
- trials: int32 [256], replicated, may hold values from 0 to 2047
Outputs:
- spectra: float32 [48, 2, 8, 256], P('chan', None, 'grp'), parts along dimension 2
- power: float32 [8, 256], P('grp', 'chan'), parts along dimension 0
The draws below stay inside these ranges and needn't reach their ends.
There are 2 independent parts, one for each index of `grp`. The reference program is written for one: setup_inputs(seed, part) draws one part's arguments, and reference() takes and returns one part's arrays. A program takes and returns all parts, laid end to end along the dimension named above; an argument that names none is the same for every part. Nothing has to cross between parts.
All inputs are finite; a program needn't handle non-finite values.
Results may differ from the reference program's by a relative error of at most 0.0037.
Values may be sent and summed in bfloat16 or wider, within the bound.
No kernel may reach another device: no remote copies, remote signals or barrier semaphores. Data moves between devices by JAX's collectives and lax.ppermute only.
A program may use at most 64 MiB of HBM per device.

```python
import math
import jax
import jax.numpy as jnp
from jax import lax

B = 4
CHANNELS = 16384
SAMPLES = 2048
SUBSTEPS = 512
TRIALS = 256
BINS = 48


def draw_delay_step(key, part):
    base_key = jax.random.fold_in(key, 4711)
    band_key, offset_key, pick_key = jax.random.split(base_key, 3)
    band_low = jax.random.randint(band_key, (), 2 * CHANNELS, 4 * CHANNELS, dtype=jnp.int32)
    channel_index = jnp.arange(CHANNELS, dtype=jnp.int32)
    frequency = band_low + channel_index
    band_top = band_low + CHANNELS
    gap_index = band_top - frequency
    scaled_gap = 4 * SAMPLES * gap_index // frequency
    coarse_delay = scaled_gap * (band_top + frequency) // (4 * frequency)
    sub_sample = jax.random.randint(offset_key, (CHANNELS,), 0, SUBSTEPS, dtype=jnp.int32)
    values = coarse_delay % SAMPLES * SUBSTEPS + sub_sample
    chosen = jax.random.randint(pick_key, (), 0, CHANNELS - 1, dtype=jnp.int32)
    values = jnp.where(channel_index == chosen, SAMPLES * SUBSTEPS - 1, values)
    values = jnp.where(channel_index == CHANNELS - 1, 0, values)
    return values.astype(jnp.int32)


def touch_ends(drawn, own_key, low, top_value):
    shape = drawn.shape
    place = [jax.random.randint(jax.random.fold_in(own_key, axis), (), 0, shape[axis]) for axis in range(len(shape))]
    drawn = drawn.at[tuple(place)].set(low)
    longest = shape.index(max(shape))
    place[longest] = (place[longest] + 1) % shape[longest]
    return drawn.at[tuple(place)].set(top_value)


def steps_of(own_key, shape, shards, smallest, top_value):
    loudness, own = 1.0, jax.random.fold_in(own_key, 6)
    for dim, shards_of in shards:
        heights = jnp.exp(jax.random.uniform(jax.random.fold_in(own, dim), (shards_of,), jnp.float32, smallest / len(shards), top_value / len(shards)))
        loudness = loudness * jnp.repeat(heights, shape[dim] // shards_of).reshape([-1 if axis == dim else 1 for axis in range(len(shape))])
    return loudness


def normal_values(stream_key, extent, spread, most, pieces=(), kind=jnp.bfloat16):
    result = spread * jax.random.normal(stream_key, extent, jnp.float32)
    if pieces:
        result = result * steps_of(stream_key, extent, pieces, -0.22, 0.18)
    return jnp.clip(result, -most, most).astype(kind)


def setup_inputs(seed: int = 0, part: int = 0) -> dict:
    key_list = jax.random.split(jax.random.key(seed), 4)
    part_splits = jax.random.split(jax.random.fold_in(key_list[3], part), 4)
    voltages = normal_values(part_splits[0], (B, CHANNELS, SAMPLES), 1.0, 6.0, ((1, 16),))
    delay_step = draw_delay_step(jax.random.fold_in(key_list[3], 71), part)
    trials = touch_ends(jax.random.randint(key_list[2], (TRIALS,), 0, SAMPLES), jax.random.fold_in(key_list[2], 1), 0, SAMPLES - 1).astype(jnp.int32)
    return dict(voltages=voltages, delay_step=delay_step, trials=trials)


def build_table(samples, bins):
    times = jnp.arange(samples, dtype=jnp.int32)
    frequency = jnp.arange(bins, dtype=jnp.int32)
    phase_index = times[:, None] * frequency[None, :] % samples
    angles = phase_index.astype(jnp.float32) * (2.0 * math.pi / samples)
    return jnp.concatenate([jnp.cos(angles), -jnp.sin(angles)], axis=1).astype(jnp.bfloat16)

def make_phases(spin_bin, delay_step, trials, modulus):
    chan_phase = spin_bin * delay_step % modulus
    phase_index = chan_phase[:, None] * trials[None, :] % modulus
    angles = phase_index.astype(jnp.float32) * (2.0 * math.pi / modulus)
    return jnp.concatenate([jnp.cos(angles), jnp.sin(angles)], axis=1)

def reference(voltages, delay_step, trials):
    modulus = SAMPLES * SUBSTEPS
    dft_table = build_table(SAMPLES, BINS).astype(jnp.float32)
    spectrum = jnp.einsum('tg,bct->gbc', dft_table, voltages.astype(jnp.float32))
    spectrum = (spectrum * (1.0 / math.sqrt(SAMPLES))).astype(jnp.bfloat16)
    spectrum = spectrum.reshape(2, BINS, B, CHANNELS)
    chan_scale = 1.0 / math.sqrt(CHANNELS)

    def one_bin(spin_bin):
        pair_rows = lax.dynamic_index_in_dim(spectrum, spin_bin, axis=1, keepdims=False).reshape(2 * B, CHANNELS)
        pair_rows = pair_rows.astype(jnp.float32)
        phases = make_phases(spin_bin, delay_step, trials, modulus)
        product = jnp.dot(pair_rows, phases, precision=lax.Precision.HIGHEST, preferred_element_type=jnp.float32)
        real_rows = product[:B]
        imag_rows = product[B:]
        real_out = real_rows[:, :TRIALS] - imag_rows[:, TRIALS:]
        imag_out = real_rows[:, TRIALS:] + imag_rows[:, :TRIALS]
        return jnp.stack([real_out, imag_out]) * chan_scale
    spectra = lax.map(one_bin, jnp.arange(BINS, dtype=jnp.int32))
    power = lax.optimization_barrier(jnp.sum(spectra * spectra, axis=(0, 1))) / BINS
    return (spectra, power)
```

```python
import math

import jax
import jax.numpy as jnp
import numpy as np
from jax import lax
from jax.experimental import pallas as pl
from jax.experimental.pallas import tpu as pltpu
from jax.sharding import PartitionSpec as P

SUBSTEPS = 512
SPIN_DEV = 3
BLOCK = 256
LANES = 128
F32 = jnp.float32
BF16 = jnp.bfloat16

N_ALPHA = 8
N_A = 8
N_B = 4


def dft_rows(samples, bins):
    times = np.arange(samples, dtype=np.int64)
    freq = np.arange(bins, dtype=np.int64)
    angle = (freq[:, None] * times[None, :] % samples).astype(np.float32) * np.float32(
        2.0 * math.pi / samples
    )
    table = np.concatenate([np.cos(angle), -np.sin(angle)], axis=0)
    return table.astype(jnp.bfloat16)


def sign_matrix():
    out = np.zeros((128, 256), np.float32)
    for lane in range(128):
        a = lane // 8 - 7.5
        b = lane % 8 - 3.5
        sa, sb = np.sign(a), np.sign(b)
        j, k = int(abs(a) - 0.5), int(abs(b) - 0.5)
        col = lambda tb, ta: k * 32 + (tb * 2 + ta) * 8 + j
        out[col(0, 0), lane] = 1.0
        out[col(1, 1), lane] = -sa * sb
        out[col(0, 1), 128 + lane] = sa
        out[col(1, 0), 128 + lane] = sb
    return np.concatenate([out, out], axis=0).astype(jnp.bfloat16)


def cos_sin(phase, modulus):
    quarter = modulus // 4
    phase = phase & (modulus - 1)
    turn = lax.shift_right_logical(phase + quarter // 2, int(math.log2(quarter)))
    rest = phase - turn * quarter
    x = rest.astype(F32) * (2.0 * math.pi / modulus)
    z = x * x
    s = x + x * z * (-1.6666654611e-1 + z * (8.3321608736e-3 - z * 1.9515295891e-4))
    c = 1.0 - 0.5 * z + z * z * (
        4.166664568298827e-2 + z * (-1.388731625493765e-3 + z * 2.443315711809948e-5)
    )
    turn = turn & 3
    odd = (turn & 1) == 1
    cos_out = jnp.where(odd, s, c)
    sin_out = jnp.where(odd, c, s)
    cos_out = jnp.where((turn == 1) | (turn == 2), -cos_out, cos_out)
    sin_out = jnp.where(turn >= 2, -sin_out, sin_out)
    return cos_out, sin_out


def phase_kernel(
    bins,
    beams,
    groups,
    delay_ref,
    trials_ref,
    table_ref,
    signs_ref,
    volt_ref,
    keep_ref,
    send_ref,
    x_ref,
    acc_ref,
    sel_ref,
    mix_ref,
):
    step = pl.program_id(0)
    steps = pl.num_programs(0)
    samples = volt_ref.shape[2]
    block = volt_ref.shape[1]
    modulus = 2 * samples * SUBSTEPS
    tiles = block // LANES
    rows8 = 2 * beams

    @pl.when(step == 0)
    def _():
        acc_ref[...] = jnp.zeros_like(acc_ref)

    scale = 1.0 / math.sqrt(samples)
    for beam in range(beams):
        part = lax.dot_general(
            table_ref[...], volt_ref[beam], (((1,), (1,)), ((), ())), preferred_element_type=F32
        )
        part = (part * scale).astype(BF16).astype(F32)
        for k in range(2):
            for t in range(tiles):
                x_ref[t, pl.ds(k * beams + beam, bins, stride=rows8), :] = part[
                    k * bins : (k + 1) * bins, t * LANES : (t + 1) * LANES
                ]

    first = (lax.axis_index("chan") * steps + step) * tiles
    delay = jnp.concatenate([delay_ref[pl.ds(first + t, 1), :] for t in range(tiles)], axis=1)
    delay = jnp.broadcast_to(delay, (8, block))
    sub = lax.broadcasted_iota(jnp.int32, (8, block), 0)
    ca1, sa1 = cos_sin(delay * (128 * (2 * sub + 1)), modulus)
    cj1, sj1 = cos_sin(delay * (8 * (2 * sub + 1)), modulus)
    mult = jnp.where(sub < N_B, 2 * sub + 1, samples - 1)
    cb1, sb1 = cos_sin(delay * mult, modulus)

    def turn(c, s, c1, s1):
        return c * c1 - s * s1, c * s1 + s * c1

    sign = jnp.where(sub < beams, -1.0, 1.0).astype(F32)

    def row(x, r):
        return jnp.broadcast_to(x[r : r + 1, :], (8, block))

    def one_bin(f, carry):
        ca, sa, cj, sj, cb, sb = carry
        base = pl.multiple_of(f * rows8, rows8)
        x = jnp.concatenate([x_ref[t, pl.ds(base, rows8), :] for t in range(tiles)], axis=1)
        z = x * row(cb, N_B) + pltpu.roll(x, beams, 0) * (sign * row(sb, N_B))
        lhs = []
        for r in range(rows8):
            zr = row(z, r)
            lhs += [zr * ca, zr * sa]
        rhs = []
        for k in range(N_B):
            c, s = row(cb, k), row(sb, k)
            rhs += [c * cj, c * sj, s * cj, s * sj]
        lhs = jnp.concatenate(lhs, axis=0).astype(BF16)
        rhs = jnp.concatenate(rhs, axis=0).astype(BF16)
        acc_ref[f] += lax.dot_general(
            lhs, rhs, (((1,), (1,)), ((), ())), preferred_element_type=F32
        )
        ca, sa = turn(ca, sa, ca1, sa1)
        cj, sj = turn(cj, sj, cj1, sj1)
        cb, sb = turn(cb, sb, cb1, sb1)
        return ca, sa, cj, sj, cb, sb

    one = jnp.ones((8, block), F32)
    zero = jnp.zeros((8, block), F32)
    lax.fori_loop(0, bins, one_bin, (one, zero, one, zero, one, zero), unroll=4)

    @pl.when(step == steps - 1)
    def _():
        half = beams * 8

        def mix(f, carry):
            g = acc_ref[f]
            plus, minus = [], []
            for b in range(beams):
                zc = g[b * 16 : b * 16 + 8]
                zs = g[b * 16 + 8 : b * 16 + 16]
                wc = g[(beams + b) * 16 : (beams + b) * 16 + 8]
                ws = g[(beams + b) * 16 + 8 : (beams + b) * 16 + 16]
                plus.append((zc - ws, zs + wc))
                minus.append((zc + ws, wc - zs))
            q = jnp.concatenate(
                [p[0] for p in plus]
                + [p[0] for p in minus]
                + [p[1] for p in plus]
                + [p[1] for p in minus],
                axis=0,
            )
            hi = q.astype(BF16)
            lo = (q - hi.astype(F32)).astype(BF16)
            u = jnp.dot(
                jnp.concatenate([hi, lo], axis=1), signs_ref[...], preferred_element_type=F32
            )
            re = u[: 2 * half, :128] - u[2 * half :, 128:]
            im = u[: 2 * half, 128:] + u[2 * half :, :128]
            base = pl.multiple_of(f * 2 * half, half)
            for s in range(2):
                sel_ref[s, pl.ds(base, half), :] = re[s * half : (s + 1) * half]
                sel_ref[s, pl.ds(base + half, half), :] = im[s * half : (s + 1) * half]
            return carry

        lax.fori_loop(0, bins, mix, 0, unroll=4)

        rows = bins * rows8
        trials = trials_ref[...]
        count = trials.shape[1]
        lane = lax.broadcasted_iota(jnp.int32, (128, count), 0)
        total = jnp.zeros((rows, count), F32)
        for s in range(2):
            for a in range(N_ALPHA):
                low = samples // 2 + 128 * a if s == 0 else samples // 2 - 128 * (a + 1)
                pick = (lane + low == trials).astype(F32).astype(BF16)
                y = sel_ref[s, pl.ds(a, rows, stride=8), :]
                hi = y.astype(BF16)
                lo = (y - hi.astype(F32)).astype(BF16)
                total += jnp.dot(
                    jnp.concatenate([hi, lo], axis=1),
                    jnp.concatenate([pick, pick], axis=0),
                    preferred_element_type=F32,
                )
        flip = total.T
        per = rows // groups
        tper = count // groups
        bins_rows = per * (count // LANES)
        for g in range(groups):
            for h in range(count // LANES):
                mix_ref[g % 2, g // 2, h * per : (h + 1) * per, :] = total[
                    g * per : (g + 1) * per, h * LANES : (h + 1) * LANES
                ]
            for m in range(rows // LANES):
                mix_ref[
                    g % 2, g // 2, bins_rows + m * tper : bins_rows + (m + 1) * tper, :
                ] = flip[g * tper : (g + 1) * tper, m * LANES : (m + 1) * LANES]
        mine = lax.rem(lax.axis_index("chan"), 2)
        keep_ref[...] = mix_ref[mine]
        send_ref[...] = mix_ref[1 - mine]


def per_device(voltages, delay_step, trials):
    beams, local_chan, samples = voltages.shape
    groups = lax.axis_size("chan")
    bins = SPIN_DEV * groups
    all_chan = delay_step.shape[0]
    count = trials.shape[0]
    chan_scale = 1.0 / math.sqrt(all_chan)
    block = min(BLOCK, local_chan)
    steps = local_chan // block
    tiles = block // LANES
    rows8 = 2 * beams
    rows = bins * rows8
    per = rows // groups
    tper = count // groups
    bins_rows = per * (count // LANES)
    out_rows = bins_rows + tper * (rows // LANES)

    table = jnp.asarray(dft_rows(samples, bins))
    signs = jnp.asarray(sign_matrix())
    full = lambda *shape: pl.BlockSpec(shape, lambda i: (0,) * len(shape))
    piece = jax.ShapeDtypeStruct((groups // 2, out_rows, LANES), F32)
    keep, send = pl.pallas_call(
        lambda *refs: phase_kernel(bins, beams, groups, *refs),
        grid=(steps,),
        in_specs=[
            full(all_chan // LANES, LANES),
            full(1, count),
            full(2 * bins, samples),
            full(256, 256),
            pl.BlockSpec((beams, block, samples), lambda i: (0, i, 0)),
        ],
        out_specs=[full(*piece.shape), full(*piece.shape)],
        out_shape=[piece, piece],
        scratch_shapes=[
            pltpu.VMEM((tiles, rows, LANES), F32),
            pltpu.VMEM((bins, 16 * rows8, 128), F32),
            pltpu.VMEM((2, rows * 8, 128), F32),
            pltpu.VMEM((2, groups // 2, out_rows, LANES), F32),
        ],
        compiler_params=pltpu.CompilerParams(
            dimension_semantics=("arbitrary",), vmem_limit_bytes=60 << 20
        ),
        name="dedisperse",
    )(
        delay_step.reshape(-1, LANES),
        trials.reshape(1, count),
        table,
        signs,
        voltages,
    )

    index = lax.axis_index("chan")
    received = lax.ppermute(send, "chan", [(i, i ^ 1) for i in range(groups)])
    own = keep + received
    bit = 2
    while bit < groups:
        own = own.reshape(-1, 2, out_rows, LANES)
        mine = (index // bit) % 2
        other = lax.dynamic_index_in_dim(own, 1 - mine, 1, keepdims=False)
        if bit == 2:
            other = other.astype(BF16)
        received = lax.ppermute(other, "chan", [(i, i ^ bit) for i in range(groups)])
        own = lax.dynamic_index_in_dim(own, mine, 1, keepdims=False) + received.astype(F32)
        bit *= 2
    own = own.reshape(out_rows, LANES) * chan_scale
    spectra = own[:bins_rows].reshape(count // LANES, per, LANES).transpose(1, 0, 2)
    spectra = spectra.reshape(SPIN_DEV, 2, beams, count)
    square = own[bins_rows:]
    square = square * square
    square = square.reshape(-1, tper, LANES // beams, beams)
    power = jnp.sum(square, axis=(0, 2)).T / bins
    return spectra, power


def solution(mesh):
    return jax.shard_map(
        per_device,
        mesh=mesh,
        in_specs=(P("grp", "chan", None), P(), P()),
        out_specs=(P("chan", None, "grp", None), P("grp", "chan")),
        check_vma=False,
    )
```

```python
import math

import jax
import jax.numpy as jnp
import numpy as np
from jax import lax
from jax.experimental import pallas as pl
from jax.experimental.pallas import tpu as pltpu
from jax.sharding import PartitionSpec as P

SUBSTEPS = 512
SPIN_DEV = 3
BLOCK = 256
LANES = 128
F32 = jnp.float32
BF16 = jnp.bfloat16

N_ALPHA = 8
N_B = 4


def dft_rows(samples, bins):
    times = np.arange(samples, dtype=np.int64)
    freq = np.arange(bins, dtype=np.int64)
    angle = (freq[:, None] * times[None, :] % samples).astype(np.float32) * np.float32(
        2.0 * math.pi / samples
    )
    table = np.concatenate([np.cos(angle), -np.sin(angle)], axis=0)
    return table.astype(jnp.bfloat16)


def sign_matrix():
    out = np.zeros((128, 256), np.float32)
    for lane in range(128):
        a = lane // 8 - 7.5
        b = lane % 8 - 3.5
        sa, sb = np.sign(a), np.sign(b)
        j, k = int(abs(a) - 0.5), int(abs(b) - 0.5)
        col = lambda tb, ta: k * 32 + (tb * 2 + ta) * 8 + j
        out[col(0, 0), lane] = 1.0
        out[col(1, 1), lane] = -sa * sb
        out[col(0, 1), 128 + lane] = sa
        out[col(1, 0), 128 + lane] = sb
    return np.concatenate([out, out], axis=0).astype(jnp.bfloat16)


def cos_sin(phase, modulus):
    quarter = modulus // 4
    phase = phase & (modulus - 1)
    turn = lax.shift_right_logical(phase + quarter // 2, int(math.log2(quarter)))
    rest = phase - turn * quarter
    x = rest.astype(F32) * (2.0 * math.pi / modulus)
    z = x * x
    s = x + x * z * (-1.6666654611e-1 + z * (8.3321608736e-3 - z * 1.9515295891e-4))
    c = 1.0 - 0.5 * z + z * z * (
        4.166664568298827e-2 + z * (-1.388731625493765e-3 + z * 2.443315711809948e-5)
    )
    turn = turn & 3
    odd = (turn & 1) == 1
    cos_out = jnp.where(odd, s, c)
    sin_out = jnp.where(odd, c, s)
    cos_out = jnp.where((turn == 1) | (turn == 2), -cos_out, cos_out)
    sin_out = jnp.where(turn >= 2, -sin_out, sin_out)
    return cos_out, sin_out


def turned(c, s, c1, s1):
    return c * c1 - s * s1, c * s1 + s * c1


def phase_kernel(
    groups,
    delay_ref,
    trials_ref,
    table_ref,
    signs_ref,
    volt_ref,
    keep_ref,
    send_ref,
    new_x_ref,
    new_b_ref,
    x_ref,
    b_ref,
    one_ref,
    acc_ref,
    sel_ref,
    mix_ref,
):
    step = pl.program_id(0)
    steps = pl.num_programs(0) - 1
    beams, block, samples = volt_ref.shape
    bins = acc_ref.shape[0]
    modulus = 2 * samples * SUBSTEPS
    tiles = block // LANES
    rows8 = 2 * beams
    scale = 1.0 / math.sqrt(samples)

    def angles():
        first = (lax.axis_index("chan") * steps + step) * tiles
        delay = jnp.concatenate([delay_ref[pl.ds(first + t, 1), :] for t in range(tiles)], axis=1)
        delay = jnp.broadcast_to(delay, (8, block))
        sub = lax.broadcasted_iota(jnp.int32, (8, block), 0)
        one_ref[0], one_ref[1] = cos_sin(delay * (128 * (2 * sub + 1)), modulus)
        one_ref[2], one_ref[3] = cos_sin(delay * (8 * (2 * sub + 1)), modulus)

        def ladder(mult):
            c, s = cos_sin(delay * (mult * sub), modulus)
            c1, s1 = cos_sin(delay * (mult * 8), modulus)
            cs, ss = [c], [s]
            for _ in range(bins // 8 - 1):
                c, s = turned(c, s, c1, s1)
                cs.append(c)
                ss.append(s)
            return jnp.concatenate(cs, axis=0), jnp.concatenate(ss, axis=0)

        for k in range(N_B):
            c, s = ladder(2 * k + 1)
            for t in range(tiles):
                lanes = slice(t * LANES, (t + 1) * LANES)
                new_b_ref[t, 2 * k] = c[:, lanes]
                new_b_ref[t, 2 * k + 1] = s[:, lanes]
        return ladder(samples - 1)

    def spectrum(beam, middle):
        part = lax.dot_general(
            volt_ref[beam], table_ref[...], (((1,), (1,)), ((), ())), preferred_element_type=F32
        ).T
        part = (part * scale).astype(BF16).astype(F32)
        zr, zi = turned(part[:bins], part[bins:], *middle)
        for t in range(tiles):
            lanes = slice(t * LANES, (t + 1) * LANES)
            new_x_ref[t, beam] = zr[:, lanes]
            new_x_ref[t, beams + beam] = zi[:, lanes]

    def spread(ref, r, f):
        return jnp.concatenate(
            [jnp.broadcast_to(ref[t, r, pl.ds(f, 1), :], (8, LANES)) for t in range(tiles)], axis=1
        )

    def take():
        x_ref[...] = new_x_ref[...]
        b_ref[...] = new_b_ref[...]
        return tuple(one_ref[n] for n in range(4))

    def some_bins(quarter, carry, unit):
        ca1, sa1, cj1, sj1 = unit

        def one_bin(f, carry):
            ca, sa, cj, sj = carry
            lhs = []
            for r in range(rows8):
                zr = spread(x_ref, r, f)
                lhs += [zr * ca, zr * sa]
            rhs = []
            for k in range(N_B):
                c, s = spread(b_ref, 2 * k, f), spread(b_ref, 2 * k + 1, f)
                rhs += [c * cj, c * sj, s * cj, s * sj]
            lhs = jnp.concatenate(lhs, axis=0).astype(BF16)
            rhs = jnp.concatenate(rhs, axis=0).astype(BF16)
            acc_ref[f] += lax.dot_general(
                lhs, rhs, (((1,), (1,)), ((), ())), preferred_element_type=F32
            )
            ca, sa = turned(ca, sa, ca1, sa1)
            cj, sj = turned(cj, sj, cj1, sj1)
            return ca, sa, cj, sj

        size = bins // 4
        return lax.fori_loop(quarter * size, (quarter + 1) * size, one_bin, carry, unroll=12)

    one = jnp.ones((8, block), F32)
    zero = jnp.zeros((8, block), F32)
    start = (one, zero, one, zero)

    def last():
        half = beams * 8

        def mix(f, carry):
            g = acc_ref[f]
            plus, minus = [], []
            for b in range(beams):
                zc = g[b * 16 : b * 16 + 8]
                zs = g[b * 16 + 8 : b * 16 + 16]
                wc = g[(beams + b) * 16 : (beams + b) * 16 + 8]
                ws = g[(beams + b) * 16 + 8 : (beams + b) * 16 + 16]
                plus.append((zc - ws, zs + wc))
                minus.append((zc + ws, wc - zs))
            q = jnp.concatenate(
                [p[0] for p in plus]
                + [p[0] for p in minus]
                + [p[1] for p in plus]
                + [p[1] for p in minus],
                axis=0,
            )
            hi = q.astype(BF16)
            lo = (q - hi.astype(F32)).astype(BF16)
            u = jnp.dot(
                jnp.concatenate([hi, lo], axis=1), signs_ref[...], preferred_element_type=F32
            )
            re = u[: 2 * half, :128] - u[2 * half :, 128:]
            im = u[: 2 * half, 128:] + u[2 * half :, :128]
            base = pl.multiple_of(f * 2 * half, half)
            for s in range(2):
                sel_ref[s, pl.ds(base, half), :] = re[s * half : (s + 1) * half]
                sel_ref[s, pl.ds(base + half, half), :] = im[s * half : (s + 1) * half]
            return carry

        lax.fori_loop(0, bins, mix, 0, unroll=48)

        rows = bins * rows8
        trials = trials_ref[...]
        count = trials.shape[1]
        lane = lax.broadcasted_iota(jnp.int32, (128, count), 0)
        every, picks = [], []
        for s in range(2):
            for a in range(N_ALPHA):
                low = samples // 2 + 128 * a if s == 0 else samples // 2 - 128 * (a + 1)
                picks.append((lane + low == trials).astype(F32).astype(BF16))
                every.append(sel_ref[s, pl.ds(a, rows, stride=8), :].astype(BF16))
        total = jnp.dot(
            jnp.concatenate(every, axis=1),
            jnp.concatenate(picks, axis=0),
            preferred_element_type=F32,
        )
        flip = total.T
        per = rows // groups
        tper = count // groups
        for g in range(groups):
            piece = [
                total[g * per : (g + 1) * per, h * LANES : (h + 1) * LANES]
                for h in range(count // LANES)
            ] + [
                flip[g * tper : (g + 1) * tper, m * LANES : (m + 1) * LANES]
                for m in range(rows // LANES)
            ]
            mix_ref[g % 2, g // 2] = jnp.concatenate(piece, axis=0).astype(mix_ref.dtype)
        mine = lax.axis_index("chan") & 1
        keep_ref[...] = mix_ref[mine]
        send_ref[...] = mix_ref[1 - mine]

    @pl.when(step == 0)
    def _():
        acc_ref[...] = jnp.zeros_like(acc_ref)
        middle = angles()
        for beam in range(beams):
            spectrum(beam, middle)

    @pl.when((step > 0) & (step < steps))
    def _():
        unit = take()
        middle = angles()
        turn = start
        for quarter in range(4):
            for beam in range(beams * quarter // 4, beams * (quarter + 1) // 4):
                spectrum(beam, middle)
            turn = some_bins(quarter, turn, unit)

    @pl.when(step == steps)
    def _():
        unit = take()
        turn = start
        for quarter in range(4):
            turn = some_bins(quarter, turn, unit)
        last()


def finish_kernel(bins, chan_scale, own_ref, received_ref, spectra_ref, power_ref):
    spin, _, beams, count = spectra_ref.shape
    tper = power_ref.shape[1]
    rows = bins * 2 * beams
    per = spin * 2 * beams
    half = lax.axis_size("chan") // 2
    mine = (lax.axis_index("chan") & half) // half
    total = (own_ref[mine] + received_ref[...]) * chan_scale
    for h in range(count // LANES):
        for f in range(spin):
            for k in range(2):
                row = h * per + (f * 2 + k) * beams
                spectra_ref[f, k, :, h * LANES : (h + 1) * LANES] = total[row : row + beams]
    first = per * (count // LANES)
    power = jnp.zeros((tper, LANES), F32)
    for m in range(rows // LANES):
        part = total[first + m * tper : first + (m + 1) * tper]
        power += part * part
    beam_of = lax.broadcasted_iota(jnp.int32, (8, LANES), 1) % beams
    pick = (beam_of == lax.broadcasted_iota(jnp.int32, (8, LANES), 0)).astype(F32)
    power = lax.dot_general(
        pick,
        power,
        (((1,), (1,)), ((), ())),
        precision=lax.Precision.HIGHEST,
        preferred_element_type=F32,
    )
    power_ref[...] = power[:beams] / bins


def per_device(voltages, delay_step, trials):
    beams, local_chan, samples = voltages.shape
    groups = lax.axis_size("chan")
    bins = SPIN_DEV * groups
    all_chan = delay_step.shape[0]
    count = trials.shape[0]
    block = min(BLOCK, local_chan)
    steps = local_chan // block
    tiles = block // LANES
    rows8 = 2 * beams
    rows = bins * rows8
    per = rows // groups
    tper = count // groups
    out_rows = per * (count // LANES) + tper * (rows // LANES)

    full = lambda *shape: pl.BlockSpec(shape, lambda i: (0,) * len(shape))
    vmem = pl.BlockSpec(memory_space=pltpu.VMEM)
    piece = jax.ShapeDtypeStruct((groups // 2, out_rows, LANES), BF16)
    keep, send = pl.pallas_call(
        lambda *refs: phase_kernel(groups, *refs),
        grid=(steps + 1,),
        in_specs=[
            full(all_chan // LANES, LANES),
            full(1, count),
            full(2 * bins, samples),
            full(256, 256),
            pl.BlockSpec(
                (beams, block, samples), lambda i: (0, jnp.minimum(i, steps - 1), 0)
            ),
        ],
        out_specs=[full(*piece.shape), full(*piece.shape)],
        out_shape=[piece, piece],
        scratch_shapes=[
            pltpu.VMEM((tiles, rows8, bins, LANES), F32),
            pltpu.VMEM((tiles, 2 * N_B, bins, LANES), F32),
            pltpu.VMEM((tiles, rows8, bins, LANES), F32),
            pltpu.VMEM((tiles, 2 * N_B, bins, LANES), F32),
            pltpu.VMEM((4, 8, block), F32),
            pltpu.VMEM((bins, 16 * rows8, 128), F32),
            pltpu.VMEM((2, rows * 8, 128), F32),
            pltpu.VMEM((2, groups // 2, out_rows, LANES), BF16),
        ],
        compiler_params=pltpu.CompilerParams(
            dimension_semantics=("arbitrary",), vmem_limit_bytes=60 << 20
        ),
        name="dedisperse",
    )(
        delay_step.reshape(-1, LANES),
        trials.reshape(1, count),
        jnp.asarray(dft_rows(samples, bins)),
        jnp.asarray(sign_matrix()),
        voltages,
    )

    index = lax.axis_index("chan")
    received = lax.ppermute(send, "chan", [(i, i ^ 1) for i in range(groups)])
    own = keep.astype(F32) + received.astype(F32)
    bit = 2
    while True:
        own = own.reshape(-1, 2, out_rows, LANES)
        mine = (index & bit) // bit
        other = lax.dynamic_index_in_dim(own, 1 - mine, 1, keepdims=False)
        if bit == 2:
            other = other.astype(BF16)
        received = lax.ppermute(other, "chan", [(i, i ^ bit) for i in range(groups)])
        if 2 * bit == groups:
            break
        own = lax.dynamic_index_in_dim(own, mine, 1, keepdims=False) + received.astype(F32)
        bit *= 2
    return pl.pallas_call(
        lambda *refs: finish_kernel(bins, 1.0 / math.sqrt(all_chan), *refs),
        in_specs=[vmem, vmem],
        out_specs=[vmem, vmem],
        out_shape=[
            jax.ShapeDtypeStruct((SPIN_DEV, 2, beams, count), F32),
            jax.ShapeDtypeStruct((beams, tper), F32),
        ],
        compiler_params=pltpu.CompilerParams(vmem_limit_bytes=4 << 20),
        name="finish",
    )(own.reshape(2, out_rows, LANES), received.reshape(out_rows, LANES))


def solution(mesh):
    return jax.shard_map(
        per_device,
        mesh=mesh,
        in_specs=(P("grp", "chan", None), P(), P()),
        out_specs=(P("chan", None, "grp", None), P("grp", "chan")),
        check_vma=False,
    )
```

```python
import math

import jax
import jax.numpy as jnp
import numpy as np
from jax import lax
from jax.experimental import pallas as pl
from jax.experimental.pallas import tpu as pltpu
from jax.sharding import PartitionSpec as P

SUBSTEPS = 512
SPIN_DEV = 3
BLOCK = 256
LANES = 128
F32 = jnp.float32
BF16 = jnp.bfloat16

N_ALPHA = 8
N_B = 4


def dft_rows(samples, bins):
    times = np.arange(samples, dtype=np.int64)
    freq = np.arange(bins, dtype=np.int64)
    angle = (freq[:, None] * times[None, :] % samples).astype(np.float32) * np.float32(
        2.0 * math.pi / samples
    )
    table = np.concatenate([np.cos(angle), -np.sin(angle)], axis=0)
    return table.astype(jnp.bfloat16)


def sign_matrix():
    out = np.zeros((128, 256), np.float32)
    for lane in range(128):
        a = lane // 8 - 7.5
        b = lane % 8 - 3.5
        sa, sb = np.sign(a), np.sign(b)
        j, k = int(abs(a) - 0.5), int(abs(b) - 0.5)
        col = lambda tb, ta: k * 32 + (tb * 2 + ta) * 8 + j
        out[col(0, 0), lane] = 1.0
        out[col(1, 1), lane] = -sa * sb
        out[col(0, 1), 128 + lane] = sa
        out[col(1, 0), 128 + lane] = sb
    return np.concatenate([out, out], axis=0).astype(jnp.bfloat16)


def cos_sin(phase, modulus):
    quarter = modulus // 4
    phase = phase & (modulus - 1)
    turn = lax.shift_right_logical(phase + quarter // 2, int(math.log2(quarter)))
    rest = phase - turn * quarter
    x = rest.astype(F32) * (2.0 * math.pi / modulus)
    z = x * x
    s = x + x * z * (-1.6666654611e-1 + z * (8.3321608736e-3 - z * 1.9515295891e-4))
    c = 1.0 - 0.5 * z + z * z * (
        4.166664568298827e-2 + z * (-1.388731625493765e-3 + z * 2.443315711809948e-5)
    )
    turn = turn & 3
    odd = (turn & 1) == 1
    cos_out = jnp.where(odd, s, c)
    sin_out = jnp.where(odd, c, s)
    cos_out = jnp.where((turn == 1) | (turn == 2), -cos_out, cos_out)
    sin_out = jnp.where(turn >= 2, -sin_out, sin_out)
    return cos_out, sin_out


def turned(c, s, c1, s1):
    return c * c1 - s * s1, c * s1 + s * c1


def phase_kernel(
    groups,
    delay_ref,
    trials_ref,
    table_ref,
    signs_ref,
    volt_ref,
    keep_ref,
    send_ref,
    new_x_ref,
    new_b_ref,
    x_ref,
    b_ref,
    one_ref,
    acc_ref,
    sel_ref,
    mix_ref,
):
    step = pl.program_id(0)
    steps = pl.num_programs(0)
    beams, block, samples = volt_ref.shape
    bins = acc_ref.shape[0]
    modulus = 2 * samples * SUBSTEPS
    tiles = block // LANES
    rows8 = 2 * beams
    scale = 1.0 / math.sqrt(samples)

    def angles():
        first = (lax.axis_index("chan") * steps + step) * tiles
        delay = jnp.concatenate([delay_ref[pl.ds(first + t, 1), :] for t in range(tiles)], axis=1)
        delay = jnp.broadcast_to(delay, (8, block))
        sub = lax.broadcasted_iota(jnp.int32, (8, block), 0)
        one_ref[0], one_ref[1] = cos_sin(delay * (128 * (2 * sub + 1)), modulus)
        one_ref[2], one_ref[3] = cos_sin(delay * (8 * (2 * sub + 1)), modulus)

        def ladder(mult):
            c, s = cos_sin(delay * (mult * sub), modulus)
            c1, s1 = cos_sin(delay * (mult * 8), modulus)
            cs, ss = [c], [s]
            for _ in range(bins // 8 - 1):
                c, s = turned(c, s, c1, s1)
                cs.append(c)
                ss.append(s)
            return jnp.concatenate(cs, axis=0), jnp.concatenate(ss, axis=0)

        for k in range(N_B):
            c, s = ladder(2 * k + 1)
            for t in range(tiles):
                lanes = slice(t * LANES, (t + 1) * LANES)
                new_b_ref[t, 2 * k] = c[:, lanes]
                new_b_ref[t, 2 * k + 1] = s[:, lanes]
        return ladder(samples - 1)

    def spectrum(beam, middle):
        many = 4
        out = lax.dot_general(
            volt_ref[beam : beam + many].reshape(many * block, samples),
            table_ref[...],
            (((1,), (1,)), ((), ())),
            preferred_element_type=F32,
        )
        for n in range(many):
            part = out[n * block : (n + 1) * block].T
            part = (part * scale).astype(BF16).astype(F32)
            zr, zi = turned(part[:bins], part[bins:], *middle)
            for t in range(tiles):
                lanes = slice(t * LANES, (t + 1) * LANES)
                new_x_ref[t, beam + n] = zr[:, lanes]
                new_x_ref[t, beams + beam + n] = zi[:, lanes]

    def spread(ref, r, f):
        return jnp.concatenate(
            [jnp.broadcast_to(ref[t, r, pl.ds(f, 1), :], (8, LANES)) for t in range(tiles)], axis=1
        )

    def take():
        x_ref[...] = new_x_ref[...]
        b_ref[...] = new_b_ref[...]
        return tuple(one_ref[n] for n in range(4))

    def some_bins(quarter, carry, unit):
        ca1, sa1, cj1, sj1 = unit

        def one_bin(f, carry):
            ca, sa, cj, sj = carry
            lhs = []
            for r in range(rows8):
                zr = spread(x_ref, r, f)
                lhs += [zr * ca, zr * sa]
            rhs = []
            for k in range(N_B):
                c, s = spread(b_ref, 2 * k, f), spread(b_ref, 2 * k + 1, f)
                rhs += [c * cj, c * sj, s * cj, s * sj]
            lhs = jnp.concatenate(lhs, axis=0).astype(BF16)
            rhs = jnp.concatenate(rhs, axis=0).astype(BF16)
            acc_ref[f] += lax.dot_general(
                lhs, rhs, (((1,), (1,)), ((), ())), preferred_element_type=F32
            )
            ca, sa = turned(ca, sa, ca1, sa1)
            cj, sj = turned(cj, sj, cj1, sj1)
            return ca, sa, cj, sj

        size = bins // 4
        return lax.fori_loop(quarter * size, (quarter + 1) * size, one_bin, carry, unroll=12)

    one = jnp.ones((8, block), F32)
    zero = jnp.zeros((8, block), F32)
    start = (one, zero, one, zero)

    def last():
        half = beams * 8

        def mix(f, carry):
            g = acc_ref[f]
            plus, minus = [], []
            for b in range(beams):
                zc = g[b * 16 : b * 16 + 8]
                zs = g[b * 16 + 8 : b * 16 + 16]
                wc = g[(beams + b) * 16 : (beams + b) * 16 + 8]
                ws = g[(beams + b) * 16 + 8 : (beams + b) * 16 + 16]
                plus.append((zc - ws, zs + wc))
                minus.append((zc + ws, wc - zs))
            q = jnp.concatenate(
                [p[0] for p in plus]
                + [p[0] for p in minus]
                + [p[1] for p in plus]
                + [p[1] for p in minus],
                axis=0,
            )
            hi = q.astype(BF16)
            lo = (q - hi.astype(F32)).astype(BF16)
            u = jnp.dot(
                jnp.concatenate([hi, lo], axis=1), signs_ref[...], preferred_element_type=F32
            )
            re = u[: 2 * half, :128] - u[2 * half :, 128:]
            im = u[: 2 * half, 128:] + u[2 * half :, :128]
            base = pl.multiple_of(f * 2 * half, half)
            for s in range(2):
                sel_ref[s, pl.ds(base, half), :] = re[s * half : (s + 1) * half]
                sel_ref[s, pl.ds(base + half, half), :] = im[s * half : (s + 1) * half]
            return carry

        lax.fori_loop(0, bins, mix, 0, unroll=48)

        rows = bins * rows8
        trials = trials_ref[...]
        count = trials.shape[1]
        lane = lax.broadcasted_iota(jnp.int32, (128, count), 0)
        every, picks = [], []
        for s in range(2):
            for a in range(N_ALPHA):
                low = samples // 2 + 128 * a if s == 0 else samples // 2 - 128 * (a + 1)
                picks.append((lane + low == trials).astype(F32).astype(BF16))
                every.append(sel_ref[s, pl.ds(a, rows, stride=8), :].astype(BF16))
        total = jnp.dot(
            jnp.concatenate(every, axis=1),
            jnp.concatenate(picks, axis=0),
            preferred_element_type=F32,
        )
        flip = total.T
        per = rows // groups
        tper = count // groups
        for g in range(groups):
            piece = [
                total[g * per : (g + 1) * per, h * LANES : (h + 1) * LANES]
                for h in range(count // LANES)
            ] + [
                flip[g * tper : (g + 1) * tper, m * LANES : (m + 1) * LANES]
                for m in range(rows // LANES)
            ]
            mix_ref[g % 2, g // 2] = jnp.concatenate(piece, axis=0).astype(mix_ref.dtype)
        mine = lax.axis_index("chan") & 1
        keep_ref[...] = mix_ref[mine]
        send_ref[...] = mix_ref[1 - mine]

    @pl.when(step == 0)
    def _():
        acc_ref[...] = jnp.zeros_like(acc_ref)
        middle = angles()
        for beam in range(0, beams, 4):
            spectrum(beam, middle)

    @pl.when(step > 0)
    def _():
        unit = take()
        middle = angles()
        turn = start
        for quarter in range(4):
            if quarter % 4 == 0:
                spectrum(quarter, middle)
            turn = some_bins(quarter, turn, unit)

    @pl.when(step == steps - 1)
    def _():
        unit = take()
        turn = start
        for quarter in range(4):
            turn = some_bins(quarter, turn, unit)
        last()


def finish_kernel(bins, chan_scale, own_ref, received_ref, spectra_ref, power_ref):
    spin, _, beams, count = spectra_ref.shape
    tper = power_ref.shape[1]
    rows = bins * 2 * beams
    per = spin * 2 * beams
    half = lax.axis_size("chan") // 2
    mine = (lax.axis_index("chan") & half) // half
    first = per * (count // LANES)
    received = received_ref[...].astype(F32)
    received = jnp.concatenate(
        [received[:first] + received[first : 2 * first], received[2 * first :]], axis=0
    )
    total = (own_ref[mine] + received) * chan_scale
    for h in range(count // LANES):
        for f in range(spin):
            for k in range(2):
                row = h * per + (f * 2 + k) * beams
                spectra_ref[f, k, :, h * LANES : (h + 1) * LANES] = total[row : row + beams]
    power = jnp.zeros((tper, LANES), F32)
    for m in range(rows // LANES):
        part = total[first + m * tper : first + (m + 1) * tper]
        power += part * part
    beam_of = lax.broadcasted_iota(jnp.int32, (8, LANES), 1) % beams
    pick = (beam_of == lax.broadcasted_iota(jnp.int32, (8, LANES), 0)).astype(F32)
    power = lax.dot_general(
        pick,
        power,
        (((1,), (1,)), ((), ())),
        precision=lax.Precision.HIGHEST,
        preferred_element_type=F32,
    )
    power_ref[...] = power[:beams] / bins


def per_device(voltages, delay_step, trials):
    beams, local_chan, samples = voltages.shape
    groups = lax.axis_size("chan")
    bins = SPIN_DEV * groups
    all_chan = delay_step.shape[0]
    count = trials.shape[0]
    block = min(BLOCK, local_chan)
    steps = local_chan // block
    tiles = block // LANES
    rows8 = 2 * beams
    rows = bins * rows8
    per = rows // groups
    tper = count // groups
    bins_rows = per * (count // LANES)
    out_rows = bins_rows + tper * (rows // LANES)

    full = lambda *shape: pl.BlockSpec(shape, lambda i: (0,) * len(shape))
    vmem = pl.BlockSpec(memory_space=pltpu.VMEM)
    piece = jax.ShapeDtypeStruct((groups // 2, out_rows, LANES), BF16)
    keep, send = pl.pallas_call(
        lambda *refs: phase_kernel(groups, *refs),
        grid=(steps,),
        in_specs=[
            full(all_chan // LANES, LANES),
            full(1, count),
            full(2 * bins, samples),
            full(256, 256),
            pl.BlockSpec((beams, block, samples), lambda i: (0, i, 0)),
        ],
        out_specs=[full(*piece.shape), full(*piece.shape)],
        out_shape=[piece, piece],
        scratch_shapes=[
            pltpu.VMEM((tiles, rows8, bins, LANES), F32),
            pltpu.VMEM((tiles, 2 * N_B, bins, LANES), F32),
            pltpu.VMEM((tiles, rows8, bins, LANES), F32),
            pltpu.VMEM((tiles, 2 * N_B, bins, LANES), F32),
            pltpu.VMEM((4, 8, block), F32),
            pltpu.VMEM((bins, 16 * rows8, 128), F32),
            pltpu.VMEM((2, rows * 8, 128), F32),
            pltpu.VMEM((2, groups // 2, out_rows, LANES), BF16),
        ],
        compiler_params=pltpu.CompilerParams(
            dimension_semantics=("arbitrary",), vmem_limit_bytes=60 << 20
        ),
        name="dedisperse",
    )(
        delay_step.reshape(-1, LANES),
        trials.reshape(1, count),
        jnp.asarray(dft_rows(samples, bins)),
        jnp.asarray(sign_matrix()),
        voltages,
    )

    index = lax.axis_index("chan")
    received = lax.ppermute(send, "chan", [(i, i ^ 1) for i in range(groups)])
    own = lax.optimization_barrier(keep.astype(F32)) + received.astype(F32)
    bit = 2
    while True:
        own = own.reshape(-1, 2, out_rows, LANES)
        mine = (index & bit) // bit
        other = lax.dynamic_index_in_dim(own, 1 - mine, 1, keepdims=False)
        if bit > 2:
            whole = other[:, :bins_rows]
            high = lax.reduce_precision(whole, exponent_bits=8, mantissa_bits=7)
            other = jnp.concatenate([high, whole - high, other[:, bins_rows:]], axis=1)
        received = lax.ppermute(
            other.astype(BF16), "chan", [(i, i ^ bit) for i in range(groups)]
        )
        if 2 * bit == groups:
            break
        received = received.astype(F32)
        if bit > 2:
            received = jnp.concatenate(
                [
                    received[:, :bins_rows] + received[:, bins_rows : 2 * bins_rows],
                    received[:, 2 * bins_rows :],
                ],
                axis=1,
            )
        own = lax.dynamic_index_in_dim(own, mine, 1, keepdims=False) + received
        bit *= 2
    return pl.pallas_call(
        lambda *refs: finish_kernel(bins, 1.0 / math.sqrt(all_chan), *refs),
        in_specs=[vmem, vmem],
        out_specs=[vmem, vmem],
        out_shape=[
            jax.ShapeDtypeStruct((SPIN_DEV, 2, beams, count), F32),
            jax.ShapeDtypeStruct((beams, tper), F32),
        ],
        compiler_params=pltpu.CompilerParams(vmem_limit_bytes=4 << 20),
        name="finish",
    )(own.reshape(2, out_rows, LANES), received.reshape(out_rows + bins_rows, LANES))


def solution(mesh):
    return jax.shard_map(
        per_device,
        mesh=mesh,
        in_specs=(P("grp", "chan", None), P(), P()),
        out_specs=(P("chan", None, "grp", None), P("grp", "chan")),
        check_vma=False,
    )
```

```python
import math

import jax
import jax.numpy as jnp
import numpy as np
from jax import lax
from jax.experimental import pallas as pl
from jax.experimental.pallas import tpu as pltpu
from jax.sharding import PartitionSpec as P

SUBSTEPS = 512
SPIN_DEV = 3
BLOCK = 256
LANES = 128
F32 = jnp.float32
BF16 = jnp.bfloat16

N_ALPHA = 8
N_B = 4


def dft_rows(samples, bins):
    times = np.arange(samples, dtype=np.int64)
    freq = np.arange(bins, dtype=np.int64)
    angle = (freq[:, None] * times[None, :] % samples).astype(np.float32) * np.float32(
        2.0 * math.pi / samples
    )
    table = np.concatenate([np.cos(angle), -np.sin(angle)], axis=0)
    return table.astype(jnp.bfloat16)


def sign_matrix():
    out = np.zeros((128, 256), np.float32)
    for lane in range(128):
        a = lane // 8 - 7.5
        b = lane % 8 - 3.5
        sa, sb = np.sign(a), np.sign(b)
        j, k = int(abs(a) - 0.5), int(abs(b) - 0.5)
        col = lambda tb, ta: k * 32 + (tb * 2 + ta) * 8 + j
        out[col(0, 0), lane] = 1.0
        out[col(1, 1), lane] = -sa * sb
        out[col(0, 1), 128 + lane] = sa
        out[col(1, 0), 128 + lane] = sb
    return np.concatenate([out, out], axis=0).astype(jnp.bfloat16)


def cos_sin(phase, modulus):
    quarter = modulus // 4
    phase = phase & (modulus - 1)
    turn = lax.shift_right_logical(phase + quarter // 2, int(math.log2(quarter)))
    rest = phase - turn * quarter
    x = rest.astype(F32) * (2.0 * math.pi / modulus)
    z = x * x
    s = x + x * z * (-1.6666654611e-1 + z * (8.3321608736e-3 - z * 1.9515295891e-4))
    c = 1.0 - 0.5 * z + z * z * (
        4.166664568298827e-2 + z * (-1.388731625493765e-3 + z * 2.443315711809948e-5)
    )
    turn = turn & 3
    odd = (turn & 1) == 1
    cos_out = jnp.where(odd, s, c)
    sin_out = jnp.where(odd, c, s)
    cos_out = jnp.where((turn == 1) | (turn == 2), -cos_out, cos_out)
    sin_out = jnp.where(turn >= 2, -sin_out, sin_out)
    return cos_out, sin_out


def turned(c, s, c1, s1):
    return c * c1 - s * s1, c * s1 + s * c1


def phase_kernel(
    groups,
    delay_ref,
    trials_ref,
    table_ref,
    signs_ref,
    volt_ref,
    keep_ref,
    send_ref,
    new_x_ref,
    new_b_ref,
    x_ref,
    b_ref,
    one_ref,
    acc_ref,
    sel_ref,
    mix_ref,
):
    step = pl.program_id(0)
    steps = pl.num_programs(0)
    beams, block, samples = volt_ref.shape
    bins = acc_ref.shape[0]
    modulus = 2 * samples * SUBSTEPS
    tiles = block // LANES
    rows8 = 2 * beams
    scale = 1.0 / math.sqrt(samples)

    def angles():
        first = (lax.axis_index("chan") * steps + step) * tiles
        delay = jnp.concatenate([delay_ref[pl.ds(first + t, 1), :] for t in range(tiles)], axis=1)
        delay = jnp.broadcast_to(delay, (8, block))
        sub = lax.broadcasted_iota(jnp.int32, (8, block), 0)
        one_ref[0], one_ref[1] = cos_sin(delay * (128 * (2 * sub + 1)), modulus)
        one_ref[2], one_ref[3] = cos_sin(delay * (8 * (2 * sub + 1)), modulus)

        def ladder(mult):
            c, s = cos_sin(delay * (mult * sub), modulus)
            c1, s1 = cos_sin(delay * (mult * 8), modulus)
            cs, ss = [c], [s]
            for _ in range(bins // 8 - 1):
                c, s = turned(c, s, c1, s1)
                cs.append(c)
                ss.append(s)
            return jnp.concatenate(cs, axis=0), jnp.concatenate(ss, axis=0)

        for k in range(N_B):
            c, s = ladder(2 * k + 1)
            for t in range(tiles):
                lanes = slice(t * LANES, (t + 1) * LANES)
                new_b_ref[t, 2 * k] = c[:, lanes]
                new_b_ref[t, 2 * k + 1] = s[:, lanes]
        return ladder(samples - 1)

    def spectrum(beam, middle):
        many = 4
        out = lax.dot_general(
            volt_ref[beam : beam + many].reshape(many * block, samples),
            table_ref[...],
            (((1,), (1,)), ((), ())),
            preferred_element_type=F32,
        )
        for n in range(many):
            part = out[n * block : (n + 1) * block].T
            part = (part * scale).astype(BF16).astype(F32)
            zr, zi = turned(part[:bins], part[bins:], *middle)
            for t in range(tiles):
                lanes = slice(t * LANES, (t + 1) * LANES)
                new_x_ref[t, beam + n] = zr[:, lanes]
                new_x_ref[t, beams + beam + n] = zi[:, lanes]

    def spread(ref, r, f):
        return jnp.concatenate(
            [jnp.broadcast_to(ref[t, r, pl.ds(f, 1), :], (8, LANES)) for t in range(tiles)], axis=1
        )

    def take():
        x_ref[...] = new_x_ref[...]
        b_ref[...] = new_b_ref[...]
        return tuple(one_ref[n] for n in range(4))

    def some_bins(quarter, carry, unit):
        ca1, sa1, cj1, sj1 = unit

        def one_bin(f, carry):
            ca, sa, cj, sj = carry
            lhs = []
            for r in range(rows8):
                zr = spread(x_ref, r, f)
                lhs += [zr * ca, zr * sa]
            rhs = []
            for k in range(N_B):
                c, s = spread(b_ref, 2 * k, f), spread(b_ref, 2 * k + 1, f)
                rhs += [c * cj, c * sj, s * cj, s * sj]
            lhs = jnp.concatenate(lhs, axis=0).astype(BF16)
            rhs = jnp.concatenate(rhs, axis=0).astype(BF16)
            acc_ref[f] += lax.dot_general(
                lhs, rhs, (((1,), (1,)), ((), ())), preferred_element_type=F32
            )
            ca, sa = turned(ca, sa, ca1, sa1)
            cj, sj = turned(cj, sj, cj1, sj1)
            return ca, sa, cj, sj

        size = bins // 4
        return lax.fori_loop(quarter * size, (quarter + 1) * size, one_bin, carry, unroll=12)

    one = jnp.ones((8, block), F32)
    zero = jnp.zeros((8, block), F32)
    start = (one, zero, one, zero)

    def last():
        half = beams * 8

        def mix(f, carry):
            g = acc_ref[f]
            plus, minus = [], []
            for b in range(beams):
                zc = g[b * 16 : b * 16 + 8]
                zs = g[b * 16 + 8 : b * 16 + 16]
                wc = g[(beams + b) * 16 : (beams + b) * 16 + 8]
                ws = g[(beams + b) * 16 + 8 : (beams + b) * 16 + 16]
                plus.append((zc - ws, zs + wc))
                minus.append((zc + ws, wc - zs))
            q = jnp.concatenate(
                [p[0] for p in plus]
                + [p[0] for p in minus]
                + [p[1] for p in plus]
                + [p[1] for p in minus],
                axis=0,
            )
            hi = q.astype(BF16)
            lo = (q - hi.astype(F32)).astype(BF16)
            u = jnp.dot(
                jnp.concatenate([hi, lo], axis=1), signs_ref[...], preferred_element_type=F32
            )
            re = u[: 2 * half, :128] - u[2 * half :, 128:]
            im = u[: 2 * half, 128:] + u[2 * half :, :128]
            base = pl.multiple_of(f * 2 * half, half)
            for s in range(2):
                sel_ref[s, pl.ds(base, half), :] = re[s * half : (s + 1) * half]
                sel_ref[s, pl.ds(base + half, half), :] = im[s * half : (s + 1) * half]
            return carry

        lax.fori_loop(0, bins, mix, 0, unroll=48)

        rows = bins * rows8
        trials = trials_ref[...]
        count = trials.shape[1]
        lane = lax.broadcasted_iota(jnp.int32, (128, count), 0)
        every, picks = [], []
        for s in range(2):
            for a in range(N_ALPHA):
                low = samples // 2 + 128 * a if s == 0 else samples // 2 - 128 * (a + 1)
                picks.append((lane + low == trials).astype(F32).astype(BF16))
                every.append(sel_ref[s, pl.ds(a, rows, stride=8), :].astype(BF16))
        total = jnp.dot(
            jnp.concatenate(every, axis=1),
            jnp.concatenate(picks, axis=0),
            preferred_element_type=F32,
        )
        flip = total.T
        per = rows // groups
        tper = count // groups
        for g in range(groups):
            piece = [
                total[g * per : (g + 1) * per, h * LANES : (h + 1) * LANES]
                for h in range(count // LANES)
            ] + [
                flip[g * tper : (g + 1) * tper, m * LANES : (m + 1) * LANES]
                for m in range(rows // LANES)
            ]
            mix_ref[g % 2, g // 2] = jnp.concatenate(piece, axis=0).astype(mix_ref.dtype)
        mine = lax.axis_index("chan") & 1
        keep_ref[...] = mix_ref[mine]
        send_ref[...] = mix_ref[1 - mine]

    @pl.when(step == 0)
    def _():
        acc_ref[...] = jnp.zeros_like(acc_ref)
        middle = angles()
        for beam in range(0, beams, 4):
            spectrum(beam, middle)

    @pl.when(step > 0)
    def _():
        unit = take()
        middle = angles()
        turn = start
        for quarter in range(4):
            if quarter % 4 == 0:
                spectrum(quarter, middle)
            turn = some_bins(quarter, turn, unit)

    @pl.when(step == steps - 1)
    def _():
        unit = take()
        turn = start
        for quarter in range(4):
            turn = some_bins(quarter, turn, unit)
        last()


def finish_kernel(bins, chan_scale, own_ref, received_ref, spectra_ref, power_ref):
    spin, _, beams, count = spectra_ref.shape
    tper = power_ref.shape[1]
    rows = bins * 2 * beams
    per = spin * 2 * beams
    half = lax.axis_size("chan") // 2
    mine = (lax.axis_index("chan") & half) // half
    first = per * (count // LANES)
    received = received_ref[...].astype(F32)
    received = jnp.concatenate(
        [received[:first] + received[first : 2 * first], received[2 * first :]], axis=0
    )
    total = (own_ref[mine] + received) * chan_scale
    for h in range(count // LANES):
        for f in range(spin):
            for k in range(2):
                row = h * per + (f * 2 + k) * beams
                spectra_ref[f, k, :, h * LANES : (h + 1) * LANES] = total[row : row + beams]
    power = jnp.zeros((tper, LANES), F32)
    for m in range(rows // LANES):
        part = total[first + m * tper : first + (m + 1) * tper]
        power += part * part
    beam_of = lax.broadcasted_iota(jnp.int32, (8, LANES), 1) % beams
    pick = (beam_of == lax.broadcasted_iota(jnp.int32, (8, LANES), 0)).astype(F32)
    power = lax.dot_general(
        pick,
        power,
        (((1,), (1,)), ((), ())),
        precision=lax.Precision.HIGHEST,
        preferred_element_type=F32,
    )
    power_ref[...] = power[:beams] / bins


def per_device(voltages, delay_step, trials):
    beams, local_chan, samples = voltages.shape
    groups = lax.axis_size("chan")
    bins = SPIN_DEV * groups
    all_chan = delay_step.shape[0]
    count = trials.shape[0]
    block = min(BLOCK, local_chan)
    steps = local_chan // block
    tiles = block // LANES
    rows8 = 2 * beams
    rows = bins * rows8
    per = rows // groups
    tper = count // groups
    bins_rows = per * (count // LANES)
    out_rows = bins_rows + tper * (rows // LANES)

    full = lambda *shape: pl.BlockSpec(shape, lambda i: (0,) * len(shape))
    vmem = pl.BlockSpec(memory_space=pltpu.VMEM)
    piece = jax.ShapeDtypeStruct((groups // 2, out_rows, LANES), BF16)
    keep, send = pl.pallas_call(
        lambda *refs: phase_kernel(groups, *refs),
        grid=(steps,),
        in_specs=[
            full(all_chan // LANES, LANES),
            full(1, count),
            full(2 * bins, samples),
            full(256, 256),
            pl.BlockSpec((beams, block, samples), lambda i: (0, i, 0)),
        ],
        out_specs=[full(*piece.shape), full(*piece.shape)],
        out_shape=[piece, piece],
        scratch_shapes=[
            pltpu.VMEM((tiles, rows8, bins, LANES), F32),
            pltpu.VMEM((tiles, 2 * N_B, bins, LANES), F32),
            pltpu.VMEM((tiles, rows8, bins, LANES), F32),
            pltpu.VMEM((tiles, 2 * N_B, bins, LANES), F32),
            pltpu.VMEM((4, 8, block), F32),
            pltpu.VMEM((bins, 16 * rows8, 128), F32),
            pltpu.VMEM((2, rows * 8, 128), F32),
            pltpu.VMEM((2, groups // 2, out_rows, LANES), BF16),
        ],
        compiler_params=pltpu.CompilerParams(
            dimension_semantics=("arbitrary",), vmem_limit_bytes=60 << 20
        ),
        name="dedisperse",
    )(
        delay_step.reshape(-1, LANES),
        trials.reshape(1, count),
        jnp.asarray(dft_rows(samples, bins)),
        jnp.asarray(sign_matrix()),
        voltages,
    )

    index = lax.axis_index("chan")
    received = lax.ppermute(send, "chan", [(i, i ^ 1) for i in range(groups)])
    own = lax.optimization_barrier(keep.astype(F32)) + received.astype(F32)
    own = own.reshape(-1, 4, out_rows, LANES)
    place = (index & 6) // 2
    parts = [
        lax.ppermute(
            lax.dynamic_index_in_dim(own, place ^ k, 1, keepdims=False).astype(BF16),
            "chan",
            [(i, i ^ (2 * k)) for i in range(groups)],
        )
        for k in range(1, 4)
    ]
    own = lax.dynamic_index_in_dim(own, place, 1, keepdims=False)
    for part in parts:
        own = own + part.astype(F32)
    bit = 8
    while True:
        own = own.reshape(-1, 2, out_rows, LANES)
        mine = (index & bit) // bit
        other = lax.dynamic_index_in_dim(own, 1 - mine, 1, keepdims=False)
        whole = other[:, :bins_rows]
        high = lax.reduce_precision(whole, exponent_bits=8, mantissa_bits=7)
        other = jnp.concatenate([high, whole - high, other[:, bins_rows:]], axis=1)
        received = lax.ppermute(
            other.astype(BF16), "chan", [(i, i ^ bit) for i in range(groups)]
        )
        if 2 * bit == groups:
            break
        received = received.astype(F32)
        received = jnp.concatenate(
            [
                received[:, :bins_rows] + received[:, bins_rows : 2 * bins_rows],
                received[:, 2 * bins_rows :],
            ],
            axis=1,
        )
        own = lax.dynamic_index_in_dim(own, mine, 1, keepdims=False) + received
        bit *= 2
    return pl.pallas_call(
        lambda *refs: finish_kernel(bins, 1.0 / math.sqrt(all_chan), *refs),
        in_specs=[vmem, vmem],
        out_specs=[vmem, vmem],
        out_shape=[
            jax.ShapeDtypeStruct((SPIN_DEV, 2, beams, count), F32),
            jax.ShapeDtypeStruct((beams, tper), F32),
        ],
        compiler_params=pltpu.CompilerParams(vmem_limit_bytes=4 << 20),
        name="finish",
    )(own.reshape(2, out_rows, LANES), received.reshape(out_rows + bins_rows, LANES))


def solution(mesh):
    return jax.shard_map(
        per_device,
        mesh=mesh,
        in_specs=(P("grp", "chan", None), P(), P()),
        out_specs=(P("chan", None, "grp", None), P("grp", "chan")),
        check_vma=False,
    )
```

```python
import math

import jax
import jax.numpy as jnp
import numpy as np
from jax import lax
from jax.experimental import pallas as pl
from jax.experimental.pallas import tpu as pltpu
from jax.sharding import PartitionSpec as P

SUBSTEPS = 512
SPIN_DEV = 3
BLOCK = 256
LANES = 128
F32 = jnp.float32
BF16 = jnp.bfloat16

N_ALPHA = 8
N_B = 4


def dft_rows(samples, bins):
    times = np.arange(samples, dtype=np.int64)
    freq = np.arange(bins, dtype=np.int64)
    angle = (freq[:, None] * times[None, :] % samples).astype(np.float32) * np.float32(
        2.0 * math.pi / samples
    )
    table = np.concatenate([np.cos(angle), -np.sin(angle)], axis=0)
    return table.astype(jnp.bfloat16)


def sign_matrix():
    out = np.zeros((128, 256), np.float32)
    for lane in range(128):
        a = lane // 8 - 7.5
        b = lane % 8 - 3.5
        sa, sb = np.sign(a), np.sign(b)
        j, k = int(abs(a) - 0.5), int(abs(b) - 0.5)
        col = lambda tb, ta: k * 32 + (tb * 2 + ta) * 8 + j
        out[col(0, 0), lane] = 1.0
        out[col(1, 1), lane] = -sa * sb
        out[col(0, 1), 128 + lane] = sa
        out[col(1, 0), 128 + lane] = sb
    return np.concatenate([out, out], axis=0).astype(jnp.bfloat16)


def cos_sin(phase, modulus):
    quarter = modulus // 4
    phase = phase & (modulus - 1)
    turn = lax.shift_right_logical(phase + quarter // 2, int(math.log2(quarter)))
    rest = phase - turn * quarter
    x = rest.astype(F32) * (2.0 * math.pi / modulus)
    z = x * x
    s = x + x * z * (-1.6666654611e-1 + z * (8.3321608736e-3 - z * 1.9515295891e-4))
    c = 1.0 - 0.5 * z + z * z * (
        4.166664568298827e-2 + z * (-1.388731625493765e-3 + z * 2.443315711809948e-5)
    )
    turn = turn & 3
    odd = (turn & 1) == 1
    cos_out = jnp.where(odd, s, c)
    sin_out = jnp.where(odd, c, s)
    cos_out = jnp.where((turn == 1) | (turn == 2), -cos_out, cos_out)
    sin_out = jnp.where(turn >= 2, -sin_out, sin_out)
    return cos_out, sin_out


def turned(c, s, c1, s1):
    return c * c1 - s * s1, c * s1 + s * c1


def phase_kernel(
    groups,
    delay_ref,
    trials_ref,
    table_ref,
    signs_ref,
    volt_ref,
    keep_ref,
    send_ref,
    new_x_ref,
    new_b_ref,
    x_ref,
    b_ref,
    one_ref,
    acc_ref,
    sel_ref,
    mix_ref,
):
    step = pl.program_id(0)
    steps = pl.num_programs(0)
    beams, block, samples = volt_ref.shape
    bins = acc_ref.shape[0]
    modulus = 2 * samples * SUBSTEPS
    tiles = block // LANES
    rows8 = 2 * beams
    scale = 1.0 / math.sqrt(samples)

    def angles():
        first = (lax.axis_index("chan") * steps + step) * tiles
        delay = jnp.concatenate([delay_ref[pl.ds(first + t, 1), :] for t in range(tiles)], axis=1)
        delay = jnp.broadcast_to(delay, (8, block))
        sub = lax.broadcasted_iota(jnp.int32, (8, block), 0)
        one_ref[0], one_ref[1] = cos_sin(delay * (128 * (2 * sub + 1)), modulus)
        one_ref[2], one_ref[3] = cos_sin(delay * (8 * (2 * sub + 1)), modulus)

        def ladder(mult):
            c, s = cos_sin(delay * (mult * sub), modulus)
            c1, s1 = cos_sin(delay * (mult * 8), modulus)
            cs, ss = [c], [s]
            for _ in range(bins // 8 - 1):
                c, s = turned(c, s, c1, s1)
                cs.append(c)
                ss.append(s)
            return jnp.concatenate(cs, axis=0), jnp.concatenate(ss, axis=0)

        for k in range(N_B):
            c, s = ladder(2 * k + 1)
            for t in range(tiles):
                lanes = slice(t * LANES, (t + 1) * LANES)
                new_b_ref[t, 2 * k] = c[:, lanes]
                new_b_ref[t, 2 * k + 1] = s[:, lanes]
        return ladder(samples - 1)

    def spectrum(beam, middle):
        many = 4
        out = lax.dot_general(
            volt_ref[beam : beam + many].reshape(many * block, samples),
            table_ref[...],
            (((1,), (1,)), ((), ())),
            preferred_element_type=F32,
        )
        for n in range(many):
            part = out[n * block : (n + 1) * block].T
            part = (part * scale).astype(BF16).astype(F32)
            zr, zi = turned(part[:bins], part[bins:], *middle)
            for t in range(tiles):
                lanes = slice(t * LANES, (t + 1) * LANES)
                new_x_ref[t, beam + n] = zr[:, lanes]
                new_x_ref[t, beams + beam + n] = zi[:, lanes]

    def spread(ref, r, f):
        return jnp.concatenate(
            [jnp.broadcast_to(ref[t, r, pl.ds(f, 1), :], (8, LANES)) for t in range(tiles)], axis=1
        )

    def take():
        x_ref[...] = new_x_ref[...]
        b_ref[...] = new_b_ref[...]
        return tuple(one_ref[n] for n in range(4))

    def some_bins(quarter, carry, unit):
        ca1, sa1, cj1, sj1 = unit

        def one_bin(f, carry):
            ca, sa, cj, sj = carry
            lhs = []
            for r in range(rows8):
                zr = spread(x_ref, r, f)
                lhs += [zr * ca, zr * sa]
            rhs = []
            for k in range(N_B):
                c, s = spread(b_ref, 2 * k, f), spread(b_ref, 2 * k + 1, f)
                rhs += [c * cj, c * sj, s * cj, s * sj]
            lhs = jnp.concatenate(lhs, axis=0).astype(BF16)
            rhs = jnp.concatenate(rhs, axis=0).astype(BF16)
            acc_ref[f] += lax.dot_general(
                lhs, rhs, (((1,), (1,)), ((), ())), preferred_element_type=F32
            )
            ca, sa = turned(ca, sa, ca1, sa1)
            cj, sj = turned(cj, sj, cj1, sj1)
            return ca, sa, cj, sj

        size = bins // 4
        return lax.fori_loop(quarter * size, (quarter + 1) * size, one_bin, carry, unroll=12)

    one = jnp.ones((8, block), F32)
    zero = jnp.zeros((8, block), F32)
    start = (one, zero, one, zero)

    def last():
        half = beams * 8

        def mix(f, carry):
            g = acc_ref[f]
            plus, minus = [], []
            for b in range(beams):
                zc = g[b * 16 : b * 16 + 8]
                zs = g[b * 16 + 8 : b * 16 + 16]
                wc = g[(beams + b) * 16 : (beams + b) * 16 + 8]
                ws = g[(beams + b) * 16 + 8 : (beams + b) * 16 + 16]
                plus.append((zc - ws, zs + wc))
                minus.append((zc + ws, wc - zs))
            q = jnp.concatenate(
                [p[0] for p in plus]
                + [p[0] for p in minus]
                + [p[1] for p in plus]
                + [p[1] for p in minus],
                axis=0,
            )
            hi = q.astype(BF16)
            lo = (q - hi.astype(F32)).astype(BF16)
            u = jnp.dot(
                jnp.concatenate([hi, lo], axis=1), signs_ref[...], preferred_element_type=F32
            )
            re = u[: 2 * half, :128] - u[2 * half :, 128:]
            im = u[: 2 * half, 128:] + u[2 * half :, :128]
            base = pl.multiple_of(f * 2 * half, half)
            for s in range(2):
                sel_ref[s, pl.ds(base, half), :] = re[s * half : (s + 1) * half]
                sel_ref[s, pl.ds(base + half, half), :] = im[s * half : (s + 1) * half]
            return carry

        lax.fori_loop(0, bins, mix, 0, unroll=48)

        rows = bins * rows8
        trials = trials_ref[...]
        count = trials.shape[1]
        lane = lax.broadcasted_iota(jnp.int32, (128, count), 0)
        every, picks = [], []
        for s in range(2):
            for a in range(N_ALPHA):
                low = samples // 2 + 128 * a if s == 0 else samples // 2 - 128 * (a + 1)
                picks.append((lane + low == trials).astype(F32).astype(BF16))
                every.append(sel_ref[s, pl.ds(a, rows, stride=8), :].astype(BF16))
        total = jnp.dot(
            jnp.concatenate(every, axis=1),
            jnp.concatenate(picks, axis=0),
            preferred_element_type=F32,
        )
        flip = total.T
        per = rows // groups
        tper = count // groups
        for g in range(groups):
            piece = [
                total[g * per : (g + 1) * per, h * LANES : (h + 1) * LANES]
                for h in range(count // LANES)
            ] + [
                flip[g * tper : (g + 1) * tper, m * LANES : (m + 1) * LANES]
                for m in range(rows // LANES)
            ]
            mix_ref[g % 2, g // 2] = jnp.concatenate(piece, axis=0).astype(mix_ref.dtype)
        mine = lax.axis_index("chan") & 1
        keep_ref[...] = mix_ref[mine]
        send_ref[...] = mix_ref[1 - mine]

    @pl.when(step == 0)
    def _():
        acc_ref[...] = jnp.zeros_like(acc_ref)
        middle = angles()
        for beam in range(0, beams, 4):
            spectrum(beam, middle)

    @pl.when(step > 0)
    def _():
        unit = take()
        middle = angles()
        turn = start
        for quarter in range(4):
            if quarter % 4 == 0:
                spectrum(quarter, middle)
            turn = some_bins(quarter, turn, unit)

    @pl.when(step == steps - 1)
    def _():
        unit = take()
        turn = start
        for quarter in range(4):
            turn = some_bins(quarter, turn, unit)
        last()


def finish_kernel(bins, half, chan_scale, own_ref, received_ref, spectra_ref, power_ref):
    spin, _, beams, count = spectra_ref.shape
    tper = power_ref.shape[1]
    rows = bins * 2 * beams
    per = spin * 2 * beams
    mine = (lax.axis_index("chan") & half) // half
    first = per * (count // LANES)
    received = received_ref[...].astype(F32)
    received = jnp.concatenate(
        [received[:first] + received[first : 2 * first], received[2 * first :]], axis=0
    )
    total = (own_ref[mine] + received) * chan_scale
    for h in range(count // LANES):
        for f in range(spin):
            for k in range(2):
                row = h * per + (f * 2 + k) * beams
                spectra_ref[f, k, :, h * LANES : (h + 1) * LANES] = total[row : row + beams]
    power = jnp.zeros((tper, LANES), F32)
    for m in range(rows // LANES):
        part = total[first + m * tper : first + (m + 1) * tper]
        power += part * part
    beam_of = lax.broadcasted_iota(jnp.int32, (8, LANES), 1) % beams
    pick = (beam_of == lax.broadcasted_iota(jnp.int32, (8, LANES), 0)).astype(F32)
    power = lax.dot_general(
        pick,
        power,
        (((1,), (1,)), ((), ())),
        precision=lax.Precision.HIGHEST,
        preferred_element_type=F32,
    )
    power_ref[...] = power[:beams] / bins


def per_device(voltages, delay_step, trials):
    beams, local_chan, samples = voltages.shape
    groups = lax.axis_size("chan")
    bins = SPIN_DEV * groups
    all_chan = delay_step.shape[0]
    count = trials.shape[0]
    block = min(BLOCK, local_chan)
    steps = local_chan // block
    tiles = block // LANES
    rows8 = 2 * beams
    rows = bins * rows8
    per = rows // groups
    tper = count // groups
    bins_rows = per * (count // LANES)
    out_rows = bins_rows + tper * (rows // LANES)

    full = lambda *shape: pl.BlockSpec(shape, lambda i: (0,) * len(shape))
    vmem = pl.BlockSpec(memory_space=pltpu.VMEM)
    piece = jax.ShapeDtypeStruct((groups // 2, out_rows, LANES), BF16)
    keep, send = pl.pallas_call(
        lambda *refs: phase_kernel(groups, *refs),
        grid=(steps,),
        in_specs=[
            full(all_chan // LANES, LANES),
            full(1, count),
            full(2 * bins, samples),
            full(256, 256),
            pl.BlockSpec((beams, block, samples), lambda i: (0, i, 0)),
        ],
        out_specs=[full(*piece.shape), full(*piece.shape)],
        out_shape=[piece, piece],
        scratch_shapes=[
            pltpu.VMEM((tiles, rows8, bins, LANES), F32),
            pltpu.VMEM((tiles, 2 * N_B, bins, LANES), F32),
            pltpu.VMEM((tiles, rows8, bins, LANES), F32),
            pltpu.VMEM((tiles, 2 * N_B, bins, LANES), F32),
            pltpu.VMEM((4, 8, block), F32),
            pltpu.VMEM((bins, 16 * rows8, 128), F32),
            pltpu.VMEM((2, rows * 8, 128), F32),
            pltpu.VMEM((2, groups // 2, out_rows, LANES), BF16),
        ],
        compiler_params=pltpu.CompilerParams(
            dimension_semantics=("arbitrary",), vmem_limit_bytes=60 << 20
        ),
        name="dedisperse",
    )(
        delay_step.reshape(-1, LANES),
        trials.reshape(1, count),
        jnp.asarray(dft_rows(samples, bins)),
        jnp.asarray(sign_matrix()),
        voltages,
    )

    index = lax.axis_index("chan")
    received = lax.ppermute(send, "chan", [(i, i ^ 1) for i in range(groups)])
    own = lax.optimization_barrier(keep.astype(F32)) + received.astype(F32)
    own = own.reshape(-1, 2, 2, 2, out_rows, LANES)
    near, far = (index & 2) // 2, (index & 8) // 8

    def share(k):
        part = lax.dynamic_index_in_dim(own, far ^ (k // 8), 1, keepdims=False)
        return lax.dynamic_index_in_dim(part, near ^ (k % 8 // 2), 2, keepdims=False)

    parts = [
        lax.ppermute(share(k).astype(BF16), "chan", [(i, i ^ k) for i in range(groups)])
        for k in (2, 8, 10)
    ]
    own = share(0)
    for part in parts:
        own = own + part.astype(F32)
    bits = [4] + [16 << n for n in range(8) if 16 << n < groups]
    for bit in bits:
        own = own.reshape(-1, 2, out_rows, LANES)
        mine = (index & bit) // bit
        other = lax.dynamic_index_in_dim(own, 1 - mine, 1, keepdims=False)
        whole = other[:, :bins_rows]
        high = lax.reduce_precision(whole, exponent_bits=8, mantissa_bits=7)
        other = jnp.concatenate([high, whole - high, other[:, bins_rows:]], axis=1)
        received = lax.ppermute(
            other.astype(BF16), "chan", [(i, i ^ bit) for i in range(groups)]
        )
        if bit == bits[-1]:
            break
        received = received.astype(F32)
        received = jnp.concatenate(
            [
                received[:, :bins_rows] + received[:, bins_rows : 2 * bins_rows],
                received[:, 2 * bins_rows :],
            ],
            axis=1,
        )
        own = lax.dynamic_index_in_dim(own, mine, 1, keepdims=False) + received
    return pl.pallas_call(
        lambda *refs: finish_kernel(bins, bits[-1], 1.0 / math.sqrt(all_chan), *refs),
        in_specs=[vmem, vmem],
        out_specs=[vmem, vmem],
        out_shape=[
            jax.ShapeDtypeStruct((SPIN_DEV, 2, beams, count), F32),
            jax.ShapeDtypeStruct((beams, tper), F32),
        ],
        compiler_params=pltpu.CompilerParams(vmem_limit_bytes=4 << 20),
        name="finish",
    )(own.reshape(2, out_rows, LANES), received.reshape(out_rows + bins_rows, LANES))


def solution(mesh):
    return jax.shard_map(
        per_device,
        mesh=mesh,
        in_specs=(P("grp", "chan", None), P(), P()),
        out_specs=(P("chan", None, "grp", None), P("grp", "chan")),
        check_vma=False,
    )
```
